256 devices in a mesh: dp: 16 (over x, y_hi, core), expert: 16 (over z, y_lo).
Axes of the slice: x: 4, y: 4 (y_hi: 2, y_lo: 2; y = y_hi * 2 + y_lo), z: 8, core: 2. Of those that a mesh axis runs over, the one named last changes fastest.
Arguments:
- tokens: bfloat16 [2048, 4096], P('expert', 'dp'), may hold values from -6 to 6
- expert_ids: int32 [2048, 8], P('expert'), may hold values from 0 to 63, all different within a row; in each aligned block of 128 rows (0 to 127, 128 to 255, ...) at most 32 rows name the same one
- gate_prob: float32 [2048, 8], P('expert'), may hold values from 0.05 to 0.35
- w_gate: bfloat16 [64, 4096, 768], P('expert', 'dp'), may hold values from -0.09375 to 0.09375
- w_up: bfloat16 [64, 4096, 768], P('expert', 'dp'), may hold values from -0.09375 to 0.09375
- w_down: bfloat16 [64, 768, 4096], P('expert', None, 'dp'), may hold values from -0.21875 to 0.21875
- grad_out: bfloat16 [2048, 4096], P('expert', 'dp'), may hold values from -6 to 6
Outputs:
- mixed: bfloat16 [2048, 4096], P('expert', 'dp')
- grad_tokens: bfloat16 [2048, 4096], P('expert', 'dp')
- grad_gate: float32 [2048, 8], P('expert')
- grad_w_gate: bfloat16 [64, 4096, 768], P('expert', 'dp')
- grad_w_up: bfloat16 [64, 4096, 768], P('expert', 'dp')
- grad_w_down: bfloat16 [64, 768, 4096], P('expert', None, 'dp')
The draws below stay inside these ranges and needn't reach their ends.
Inputs may be any that keep to these rules, and one draw needn't show every extreme that they name: `expert_ids`: each row names 8 different experts. Within the rows of one index of expert (aligned blocks of 128 rows) no expert is named by more than 32 rows, a bound that some block reaches.
All inputs are finite; a program needn't handle non-finite values.
Results may differ from the reference program's by a relative error of at most 0.035.
Values may be sent and summed in bfloat16 or wider, within the bound.
No kernel may reach another device: no remote copies, remote signals or barrier semaphores. Data moves between devices by JAX's collectives and lax.ppermute only.
A program may use at most 128 MiB of HBM per device.

```python
import math
import jax
import jax.numpy as jnp
import numpy as np
from jax import lax

D = 4096
FF = 768
TOPK = 8
TOK_COL = 128
EXPERTS = 64
TOKENS = 2048
CAP = 32
N_DP = 16
N_EXPERT = 16


def block_scale(own_key, extent, shards, least, largest):
    def one(axis_at, blocks):
        draws = jax.random.uniform(jax.random.fold_in(jax.random.fold_in(own_key, 6), axis_at), (blocks,), jnp.float32, least / len(shards), largest / len(shards))
        return jnp.repeat(jnp.exp(draws), extent[axis_at] // blocks).reshape((-1,) + (1,) * (len(extent) - axis_at - 1))

    level = one(*shards[0])
    for cut in shards[1:]:
        level = level * one(*cut)
    return level


def routed_block(own_key, own, number, rows, number_of, top, most, slope):
    sequence = jax.random.permutation(own_key, number_of)
    heavy_load, common = shares(number_of, rows * top, most, slope, True), shares(number_of, rows * top, most, slope, False)
    places = jnp.arange(number_of)

    def named(tallies, rotation):
        used = int((tallies > 0).sum())
        fixed = max(1, used // 4)
        shifted = fixed + (places - fixed + rotation * (used - fixed)) % max(1, number_of - fixed)
        return jnp.zeros((number_of,), jnp.int32).at[sequence[jnp.where(places < fixed, places, shifted)]].set(jnp.asarray(tallies, jnp.int32))

    tallies = jnp.where(number % 4 == 0, named(heavy_load, number // 4), named(common, number - number // 4 - 1))
    mixed = jax.random.permutation(jax.random.fold_in(own, 3), number_of)
    donor, taker = mixed[0:number_of // 2 * 2:2], mixed[1:number_of // 2 * 2:2]
    margin = jnp.minimum(tallies[donor] - 1, most - tallies[taker]) // 2
    margin = jnp.where((donor == sequence[0]) | (taker == sequence[0]) | (tallies[taker] == 0), 0, jnp.maximum(margin, 0))
    shifted = jax.random.randint(jax.random.fold_in(own, 4), (number_of // 2,), 0, 1 << 20) % (margin + 1)
    tallies = tallies.at[donor].add(-shifted).at[taker].add(shifted)
    labels = jnp.searchsorted(jnp.cumsum(tallies), jnp.arange(rows * top), side="right").astype(jnp.int32)
    grid = labels.reshape(top, rows).T
    grid = grid[jax.random.permutation(jax.random.fold_in(own, 1), rows)]
    rotation = jax.random.randint(jax.random.fold_in(own, 2), (rows, 1), 0, top)
    return jnp.take_along_axis(grid, (jnp.arange(top)[None, :] + rotation) % top, axis=1)


def shares(amount, total, limit, lean, full):
    loads = [(1 << 20) // math.isqrt(grade ** lean) + 1 for grade in range(1, amount + 1)]
    largest = limit if full else min(limit, max(-(-total // amount), total * loads[0] // sum(loads)))
    least = 1 if total - largest >= amount - 1 else 0
    counts, rest = [largest] + [least] * (amount - 1), total - largest - least * (amount - 1)
    while rest > 0:
        movable = [i for i in range(1, amount) if counts[i] < largest] or [i for i in range(1, amount) if counts[i] < limit]
        whole, remaining = sum([loads[i] for i in movable]), rest
        for i in movable:
            extra = min(limit - counts[i], max(1, remaining * loads[i] // whole), rest)
            counts[i] = counts[i] + extra
            rest = rest - extra
    return np.array(counts)


def scatter_about(key, dims, width, reach, cuts=(), kind=jnp.bfloat16):
    values = jax.random.normal(key, dims, jnp.float32) * width
    if len(cuts) > 0:
        values = block_scale(key, dims, cuts, -0.22, 0.18) * values
    return jnp.clip(values, min=-reach, max=reach).astype(kind)


def setup_inputs(seed: int = 0) -> dict:
    streams_of = jax.random.split(jax.random.key(seed), 8)
    tokens = scatter_about(streams_of[0], (TOKENS, D), 1.0, 6.0, ((0, 16), (1, 16)))
    expert_ids_keys = jax.random.split(jax.random.fold_in(streams_of[1], 1), TOKENS // TOK_COL)
    expert_ids_turns = jax.random.permutation(jax.random.fold_in(streams_of[1], 3), TOKENS // TOK_COL)
    expert_ids = jax.vmap(lambda own, number: routed_block(jax.random.fold_in(streams_of[1], 2), own, number, TOK_COL, EXPERTS, TOPK, CAP, 2))(expert_ids_keys, expert_ids_turns).reshape((TOKENS, TOPK))
    gate_prob = jnp.clip(0.05 + 0.29999999 * jax.random.uniform(streams_of[2], (TOKENS, TOPK), jnp.float32) ** block_scale(streams_of[2], (TOKENS, TOPK), ((0, 16),), -0.2, 0.2), 0.05, 0.35)
    w_gate = scatter_about(streams_of[3], (EXPERTS, D, FF), D ** -0.5, 0.09375, ((0, 16), (1, 16)))
    w_up = scatter_about(streams_of[4], (EXPERTS, D, FF), D ** -0.5, 0.09375, ((0, 16), (1, 16)))
    w_down = scatter_about(streams_of[5], (EXPERTS, FF, D), FF ** -0.5, 0.21875, ((0, 16), (2, 16)))
    grad_out = scatter_about(streams_of[6], (TOKENS, D), 1.0, 6.0, ((0, 16), (1, 16)))
    return {"tokens": tokens, "expert_ids": expert_ids, "gate_prob": gate_prob, "w_gate": w_gate, "w_up": w_up, "w_down": w_down, "grad_out": grad_out}


def sliced_sum(row_slices, weight_slices):
    parts = jnp.einsum("mrd,rdf->rmf", row_slices.astype(jnp.float32), weight_slices.astype(jnp.float32))
    rounded = lax.optimization_barrier(parts.astype(jnp.bfloat16))
    return jnp.sum(rounded.astype(jnp.float32), axis=0)


def reference(tokens, expert_ids, gate_prob, w_gate, w_up, w_down, grad_out):
    tok_count = tokens.shape[0]
    flat_ids = expert_ids.reshape(-1).astype(jnp.int32)
    assign_count = flat_ids.shape[0]
    most_rows = N_EXPERT * CAP
    slice_width = D // N_DP
    gate_flat = gate_prob.reshape(-1)
    positions = jnp.arange(most_rows, dtype=jnp.int32)

    def per_expert(carry, expert):
        mixed_acc, grad_acc, gate_acc = carry
        chosen = flat_ids == expert
        picked = jnp.nonzero(chosen, size=most_rows, fill_value=0)[0].astype(jnp.int32)
        filled = positions < jnp.sum(chosen.astype(jnp.int32))
        tok_idx = picked // TOPK
        x_rows = jnp.where(filled[:, None], tokens[tok_idx], jnp.zeros((), jnp.bfloat16))
        dy_rows = grad_out[tok_idx].astype(jnp.float32)
        gates = jnp.where(filled, gate_flat[picked], jnp.zeros((), jnp.float32))
        scaled_grad = (gates[:, None] * dy_rows).astype(jnp.bfloat16)
        wg = w_gate[expert]
        wu = w_up[expert]
        wd = w_down[expert]
        x_slices = x_rows.reshape(most_rows, N_DP, slice_width)
        gate_pre = sliced_sum(x_slices, wg.reshape(N_DP, slice_width, FF))
        up_pre = sliced_sum(x_slices, wu.reshape(N_DP, slice_width, FF))
        hidden = (jax.nn.silu(gate_pre) * up_pre).astype(jnp.bfloat16)
        expert_out = jnp.dot(hidden, wd, preferred_element_type=jnp.float32).astype(jnp.bfloat16)
        grad_slices = scaled_grad.reshape(most_rows, N_DP, slice_width)
        down_slices = jnp.transpose(wd.reshape(FF, N_DP, slice_width), (1, 2, 0))
        hidden_grad = sliced_sum(grad_slices, down_slices)
        sigmoid_g = jax.nn.sigmoid(gate_pre)
        gate_grad = (hidden_grad * up_pre * sigmoid_g * (1.0 + gate_pre * (1.0 - sigmoid_g))).astype(jnp.bfloat16)
        up_grad = (hidden_grad * gate_pre * sigmoid_g).astype(jnp.bfloat16)
        token_part = (jnp.dot(gate_grad, wg.T, preferred_element_type=jnp.float32)
                      + jnp.dot(up_grad, wu.T, preferred_element_type=jnp.float32)).astype(jnp.bfloat16)
        dw_gate = jnp.dot(x_rows.T, gate_grad, preferred_element_type=jnp.float32).astype(jnp.bfloat16)
        dw_up = jnp.dot(x_rows.T, up_grad, preferred_element_type=jnp.float32).astype(jnp.bfloat16)
        dw_down = jnp.dot(hidden.T, scaled_grad, preferred_element_type=jnp.float32).astype(jnp.bfloat16)
        out_float = expert_out.astype(jnp.float32)
        mixed_acc = mixed_acc.at[tok_idx].add(gates[:, None] * out_float)
        grad_acc = grad_acc.at[tok_idx].add(jnp.where(filled[:, None], token_part.astype(jnp.float32), jnp.zeros((), jnp.float32)))
        dots = jnp.sum(out_float * dy_rows, axis=1)
        gate_acc = gate_acc.at[picked].add(jnp.where(filled, dots, jnp.zeros((), jnp.float32)))
        return (mixed_acc, grad_acc, gate_acc), (dw_gate, dw_up, dw_down)

    start = (jnp.zeros((tok_count, D), jnp.float32), jnp.zeros((tok_count, D), jnp.float32),
             jnp.zeros((assign_count,), jnp.float32))
    final, stacked = lax.scan(per_expert, start, jnp.arange(EXPERTS, dtype=jnp.int32))
    mixed_acc, grad_acc, gate_acc = final
    grad_w_gate, grad_w_up, grad_w_down = stacked
    mixed = mixed_acc.astype(jnp.bfloat16)
    grad_tokens = grad_acc.astype(jnp.bfloat16)
    grad_gate = gate_acc.reshape(tok_count, TOPK)
    return mixed, grad_tokens, grad_gate, grad_w_gate, grad_w_up, grad_w_down
```

```python
import jax
import jax.numpy as jnp
from jax import lax
from jax.experimental import pallas as pl
from jax.experimental.pallas import tpu as pltpu
from jax.sharding import PartitionSpec as P

CONTRACT_LAST = (((1,), (1,)), ((), ()))


def gate_up_kernel(own_ref, other_ref, w_own_ref, w_other_ref, out_ref):
    rows = own_ref.shape[0] * own_ref.shape[2]
    own = own_ref[...].reshape(rows, own_ref.shape[3])
    other = other_ref[...].reshape(rows, other_ref.shape[3])
    total = jnp.dot(own, w_own_ref[0], preferred_element_type=jnp.float32)
    total = total + jnp.dot(other, w_other_ref[0], preferred_element_type=jnp.float32)
    out_ref[...] = total.astype(out_ref.dtype).reshape(out_ref.shape)


def gate_up_partials(own, other, w_own, w_other, chips):
    blocks, half, cap, width = own.shape
    wide = w_own.shape[2]
    tile = wide // 2 if wide % 256 == 0 else wide
    rows = blocks * cap
    row_spec = pl.BlockSpec((blocks, 1, cap, width), lambda e, f: (0, e, 0, 0))
    w_spec = pl.BlockSpec((1, width, tile), lambda e, f: (e, 0, f))
    return pl.pallas_call(
        gate_up_kernel,
        out_shape=jax.ShapeDtypeStruct((chips, half, rows // chips, wide), own.dtype),
        grid=(half, wide // tile),
        in_specs=[row_spec, row_spec, w_spec, w_spec],
        out_specs=pl.BlockSpec((chips, 1, rows // chips, tile), lambda e, f: (0, e, 0, f)),
        cost_estimate=pl.CostEstimate(
            flops=4 * half * rows * width * wide,
            bytes_accessed=4 * half * (rows * width + width * wide) + 2 * half * rows * wide,
            transcendentals=0,
        ),
        compiler_params=pltpu.CompilerParams(vmem_limit_bytes=32 * 1024 * 1024),
        name="gate_up_partials",
    )(own, other, w_own, w_other)


def slot_grad_kernel(got_ref, w_own_ref, w_other_ref, own_ref, other_ref):
    wide = w_own_ref.shape[2]
    rows = got_ref.shape[0] * got_ref.shape[2]
    got = got_ref[:, :, :, :wide].reshape(rows, wide)
    for w_ref, out_ref in ((w_other_ref, other_ref), (w_own_ref, own_ref)):
        total = lax.dot_general(got, w_ref[0], CONTRACT_LAST, preferred_element_type=jnp.float32)
        out_ref[0] = total.astype(out_ref.dtype)


def slot_grads(got, w_own, w_other):
    chips, half, share, padded = got.shape
    width, wide = w_own.shape[1:]
    rows = chips * share
    w_spec = pl.BlockSpec((1, width, wide), lambda e: (e, 0, 0))
    out_spec = pl.BlockSpec((1, rows, width), lambda e: (e, 0, 0))
    out = jax.ShapeDtypeStruct((half, rows, width), got.dtype)
    return pl.pallas_call(
        slot_grad_kernel,
        out_shape=(out, out),
        grid=(half,),
        in_specs=[
            pl.BlockSpec((chips, 1, share, padded), lambda e: (0, e, 0, 0)),
            w_spec,
            w_spec,
        ],
        out_specs=(out_spec, out_spec),
        cost_estimate=pl.CostEstimate(
            flops=4 * half * rows * width * wide,
            bytes_accessed=2 * half * rows * padded + 4 * half * (width * wide + rows * width),
            transcendentals=0,
        ),
        compiler_params=pltpu.CompilerParams(vmem_limit_bytes=32 * 1024 * 1024),
        name="slot_grads",
    )(got, w_own, w_other)


def three_pieces(value):
    high = lax.reduce_precision(value, 8, 7)
    rest = value - high
    middle = lax.reduce_precision(rest, 8, 7)
    low = rest - middle
    return [piece.astype(jnp.bfloat16) for piece in (high, middle, low)]


def after(value, earlier):
    return lax.optimization_barrier((value, earlier))[0]


def spread(block, axis_name, size, groups=None):
    copies = jnp.broadcast_to(block[None], (size,) + block.shape)
    return lax.all_to_all(copies, axis_name, 0, 0, tiled=True, axis_index_groups=groups)


def on_device(tokens, expert_ids, gate_prob, w_gate, w_up, w_down, grad_out):
    bf16, f32 = jnp.bfloat16, jnp.float32
    tok, fanout = expert_ids.shape
    n_exp, width, ff = w_gate.shape
    cols = lax.axis_size("expert")
    parties = lax.axis_size("dp")
    cap = 2 * tok * fanout // (n_exp * cols)
    half = n_exp // 2
    chips = parties // 2
    per_share = cols // chips
    share = per_share * cap
    core = lax.axis_index("dp") % 2
    col = lax.axis_index("expert")
    mine, theirs = core * half, (1 - core) * half
    pairs = [(i, i ^ 1) for i in range(parties)]
    same_core = [[i for i in range(parties) if i % 2 == c] for c in (0, 1)]

    levels = cols // 2
    level = col // 2

    def shifted(value, step):
        steps = [(i, (i + 2 * step) % cols) for i in range(cols)]
        return lax.ppermute(value, "expert", steps)

    def swap(value):
        return lax.ppermute(value, "dp", pairs)

    def pick(value, start, axis):
        return lax.dynamic_slice_in_dim(value, start, half, axis)

    with jax.named_scope("send_tokens"):
        routing = jnp.concatenate(
            [expert_ids.T.astype(bf16)] + three_pieces(gate_prob.T), axis=0
        )
        lanes = width // tok
        extra_rows = routing.shape[0] // lanes
        routing = jnp.concatenate(
            [routing[i * extra_rows : (i + 1) * extra_rows] for i in range(lanes)], axis=1
        )
        got_tokens = spread(jnp.concatenate([tokens, routing], axis=0), "expert", cols)
    with jax.named_scope("send_grads"):
        beside = lax.ppermute(grad_out, "expert", [(i, i ^ 1) for i in range(cols)])
        grad_pair = jnp.stack([jnp.where(col % 2 == 0, grad_out, beside), jnp.where(col % 2 == 0, beside, grad_out)])

    with jax.named_scope("swap_weights"):
        w_gate_up = jnp.concatenate([w_gate, w_up], axis=2)
        wgu_mine = pick(w_gate_up, mine, 0)
        wgu_theirs = swap(pick(w_gate_up, theirs, 0))
        wd = jnp.concatenate([pick(w_down, mine, 0), swap(pick(w_down, theirs, 0))], axis=2)

    with jax.named_scope("tables"):
        got_tokens = after(got_tokens, beside)
        all_tokens = got_tokens[:, :tok]
        packed = got_tokens[:, tok:].astype(f32)
        packed = jnp.concatenate([packed[:, :, i * tok : (i + 1) * tok] for i in range(lanes)], axis=1)
        ids = packed[:, :fanout]
        gates = packed[:, fanout : 2 * fanout]
        gates = gates + packed[:, 2 * fanout : 3 * fanout] + packed[:, 3 * fanout :]
        names = (col * n_exp + jnp.arange(n_exp)).astype(f32)
        chosen = ids[:, None] == names[None, :, None, None]
        hit = jnp.sum(chosen.astype(f32), axis=2)
        gate_of = jnp.sum(jnp.where(chosen, gates[:, None], 0.0), axis=2)
        earlier = (jnp.arange(tok)[:, None] < jnp.arange(tok)[None, :]).astype(bf16)
        rank = jnp.einsum("sea,at->set", hit.astype(bf16), earlier, preferred_element_type=f32)
        placed = (rank[:, :, None] == jnp.arange(cap, dtype=f32)[None, None, :, None]) & (
            hit[:, :, None] > 0.5
        )
        slots = placed.astype(bf16)
        gate_slots = jnp.sum(jnp.where(placed, gate_of[:, :, None], 0.0), axis=3)

    def dispatch(source):
        return jnp.einsum(
            "sqt,std->sqd",
            slots.reshape(cols, n_exp * cap, tok),
            source,
            preferred_element_type=f32,
        ).reshape(cols, n_exp, cap, width)

    def join_rows(own, other):
        rows = jnp.concatenate([own, other], axis=3).transpose(1, 0, 2, 3)
        return rows.reshape(half, cols * cap, 2 * width)

    def shares(part):
        return lax.all_to_all(part, "dp", 0, 0, tiled=True, axis_index_groups=same_core)

    def chunks(part):
        part = part.astype(bf16).reshape(half, chips, share, part.shape[-1])
        return part.transpose(1, 0, 2, 3)

    def total(got):
        return jnp.sum(got.astype(f32), axis=0)

    def in_rows(got):
        return got.transpose(1, 0, 2, 3).reshape(half, chips * share, got.shape[-1])

    with jax.named_scope("gate_up"):
        x_all = dispatch(all_tokens).astype(bf16)
        x_mine = pick(x_all, mine, 1)
        x_theirs = swap(pick(x_all, theirs, 1))
        part = gate_up_partials(x_mine, x_theirs, wgu_mine, wgu_theirs, chips)
        x_rows = join_rows(x_mine, x_theirs)
        got_gate_up = shares(part)
        gate_up = total(got_gate_up)
        gate_pre, up_pre = gate_up[..., :ff], gate_up[..., ff:]
        sigmoid_g = jax.nn.sigmoid(gate_pre)
        hidden = (gate_pre * sigmoid_g * up_pre).astype(bf16)
        got_hidden = spread(hidden, "dp", chips, same_core)
        grad_pair = after(grad_pair, part)

    with jax.named_scope("all_grads"):
        all_grads = jnp.zeros((cols, tok, width), bf16)
        for step in range(levels):
            piece = shifted(grad_pair, step) if step else grad_pair
            start = 2 * ((level + levels - step) % levels)
            all_grads = lax.dynamic_update_slice_in_dim(all_grads, piece, start, 0)

    with jax.named_scope("hidden_grad"):
        g_all = (dispatch(all_grads) * gate_slots[..., None]).astype(bf16)
        g_rows = join_rows(pick(g_all, mine, 1), swap(pick(g_all, theirs, 1)))
        part = chunks(jnp.einsum("erd,efd->erf", g_rows, wd, preferred_element_type=f32))
        got = shares(after(part, got_hidden))
        hidden_grad = total(got)
    with jax.named_scope("hidden"):
        all_hidden = in_rows(got_hidden)
    slots_mine = pick(slots, mine, 1)
    slots_theirs = pick(slots, theirs, 1)

    def combine(own, other):
        def part(slot, value):
            return jnp.einsum("sert,esrd->std", slot, value, preferred_element_type=f32)

        shape = (half, cols, cap, width)
        other = swap(other.reshape(shape))
        return (part(slots_mine, own.reshape(shape)) + part(slots_theirs, other)).astype(bf16)

    with jax.named_scope("mixed"):
        expert_out = jnp.einsum("erf,efd->erd", all_hidden, wd, preferred_element_type=f32)
        row_gates = pick(gate_slots, mine, 1).transpose(1, 0, 2).reshape(half, cols * cap)
        out_rows = (expert_out * row_gates[..., None]).astype(bf16)
        mixed_parts = combine(out_rows[..., :width], out_rows[..., width:])
        by_level = mixed_parts.reshape(levels, 2, tok, width)

        def at_level(step):
            return lax.dynamic_index_in_dim(by_level, (level + step) % levels, 0, keepdims=False)

        arrived = [at_level(0)] + [shifted(at_level(step), step) for step in range(1, levels)]
        level_sum = sum(piece.astype(f32) for piece in arrived).astype(bf16)
        even = col % 2 == 0
        keep = jnp.where(even, level_sum[0], level_sum[1])
        give = jnp.where(even, level_sum[1], level_sum[0])
        take = lax.ppermute(give, "expert", [(i, i ^ 1) for i in range(cols)])
        mixed = (keep.astype(f32) + take.astype(f32)).astype(bf16)

    with jax.named_scope("local_grads"):
        gate_grad = (hidden_grad * up_pre * sigmoid_g * (1.0 + gate_pre * (1.0 - sigmoid_g))).astype(bf16)
        up_grad = (hidden_grad * gate_pre * sigmoid_g).astype(bf16)
        my_gates = lax.dynamic_slice_in_dim(
            pick(gate_slots, mine, 1), lax.axis_index("dp") // 2 * per_share, per_share, 0
        ).transpose(1, 0, 2).reshape(half, share)
        dots = jnp.sum(hidden.astype(f32) * hidden_grad, axis=2)
        dots = jnp.where(my_gates > 0, dots / jnp.where(my_gates > 0, my_gates, 1.0), 0.0)
        tail = jnp.stack(three_pieces(dots), axis=-1)
        tail = jnp.pad(tail, ((0, 0), (0, 0), (0, 128 - tail.shape[-1])))
        local_grads = after(jnp.concatenate([gate_grad, up_grad, tail], axis=2), mixed_parts)
        got_grads = spread(local_grads, "dp", chips, same_core)

    with jax.named_scope("grad_tokens"):
        got_grads = after(got_grads, by_level)
        grad_parts = combine(*slot_grads(got_grads, wgu_mine, wgu_theirs))

    with jax.named_scope("grad_gate"):
        all_dots = got_grads[..., 2 * ff : 2 * ff + 3].astype(f32)
        all_dots = (all_dots[..., 0] + all_dots[..., 1] + all_dots[..., 2]).transpose(1, 0, 2)
        all_dots = all_dots.reshape(half, cols, cap)
        their_dots = swap(all_dots)
        first = jnp.where(core == 0, all_dots, their_dots)
        second = jnp.where(core == 0, their_dots, all_dots)
        slot_dots = jnp.concatenate([first, second], axis=0).transpose(1, 0, 2)
        dot_of = jnp.sum(jnp.where(placed, slot_dots[..., None], 0.0), axis=2)
        dot_rows = jnp.concatenate(three_pieces(dot_of), axis=1)
        dot_rows = jnp.pad(dot_rows, ((0, 0), (0, 16 - dot_rows.shape[1]), (0, 0)))
        dot_rows = jnp.concatenate([dot_rows[:, :8], dot_rows[:, 8:]], axis=2)

    with jax.named_scope("return"):
        sent = after(jnp.concatenate([grad_parts, dot_rows], axis=1), mixed)
        back = lax.all_to_all(sent, "expert", 0, 0, tiled=True)
        grad_tokens = jnp.sum(back[:, :tok].astype(f32), axis=0).astype(bf16)
        got_dots = back[:, tok:].astype(f32)
        got_dots = jnp.concatenate([got_dots[..., :tok], got_dots[..., tok:]], axis=1)
        got_dots = (
            got_dots[:, :n_exp] + got_dots[:, n_exp : 2 * n_exp] + got_dots[:, 2 * n_exp : 3 * n_exp]
        ).reshape(cols * n_exp, tok)
        picked = expert_ids.T[:, None] == jnp.arange(cols * n_exp, dtype=expert_ids.dtype)[None, :, None]
        grad_gate = jnp.sum(jnp.where(picked, got_dots[None], 0.0), axis=1).T
        gu_grads = in_rows(after(got_grads, sent)[..., : 2 * ff])

    def both_halves(own, other):
        out = jnp.zeros((n_exp,) + own.shape[1:], own.dtype)
        out = lax.dynamic_update_slice_in_dim(out, own, mine, 0)
        return lax.dynamic_update_slice_in_dim(out, other, theirs, 0)

    with jax.named_scope("weight_grads"):
        dgu = jnp.einsum("erd,erf->edf", x_rows, gu_grads, preferred_element_type=f32).astype(bf16)
        dd = jnp.einsum("erf,erd->efd", all_hidden, g_rows, preferred_element_type=f32).astype(bf16)
        dgu_other = swap(dgu[:, width:])
        dd_other = swap(dd[..., width:])
        grad_w_gate = both_halves(dgu[:, :width, :ff], dgu_other[..., :ff])
        grad_w_up = both_halves(dgu[:, :width, ff:], dgu_other[..., ff:])
        grad_w_down = both_halves(dd[..., :width], dd_other)
    return (mixed, grad_tokens, grad_gate, grad_w_gate, grad_w_up, grad_w_down)


def solution(mesh):
    return jax.shard_map(
        on_device,
        mesh=mesh,
        in_specs=(
            P("expert", "dp"),
            P("expert", None),
            P("expert", None),
            P("expert", "dp", None),
            P("expert", "dp", None),
            P("expert", None, "dp"),
            P("expert", "dp"),
        ),
        out_specs=(
            P("expert", "dp"),
            P("expert", "dp"),
            P("expert", None),
            P("expert", "dp", None),
            P("expert", "dp", None),
            P("expert", None, "dp"),
        ),
        check_vma=False,
    )
```

```python
import functools

import jax
import jax.numpy as jnp
from jax import lax
from jax.experimental import pallas as pl
from jax.experimental.pallas import tpu as pltpu
from jax.sharding import PartitionSpec as P

CONTRACT_LAST = (((1,), (1,)), ((), ()))
CONTRACT_INNER = (((1,), (0,)), ((), ()))


def partials_kernel(contract, own_ref, other_ref, w_own_ref, w_other_ref, out_ref):
    rows = own_ref.shape[0] * own_ref.shape[2]
    own = own_ref[...].reshape(rows, own_ref.shape[3])
    other = other_ref[...].reshape(rows, other_ref.shape[3])
    total = lax.dot_general(own, w_own_ref[0], contract, preferred_element_type=jnp.float32)
    total = total + lax.dot_general(
        other, w_other_ref[0], contract, preferred_element_type=jnp.float32
    )
    out_ref[...] = total.astype(out_ref.dtype).reshape(out_ref.shape)


def partials(own, other, w_own, w_other, chips, width_last):
    blocks, half, cap, width = own.shape
    wide = w_own.shape[1] if width_last else w_own.shape[2]
    tile = wide // 3 if wide % 384 == 0 else wide
    rows = blocks * cap
    row_spec = pl.BlockSpec((blocks, 1, cap, width), lambda e, f: (0, e, 0, 0))
    if width_last:
        w_spec = pl.BlockSpec((1, tile, width), lambda e, f: (e, f, 0))
    else:
        w_spec = pl.BlockSpec((1, width, tile), lambda e, f: (e, 0, f))
    return pl.pallas_call(
        functools.partial(partials_kernel, CONTRACT_LAST if width_last else CONTRACT_INNER),
        out_shape=pltpu.HBM((chips, half, rows // chips, wide), own.dtype),
        grid=(half, wide // tile),
        in_specs=[row_spec, row_spec, w_spec, w_spec],
        out_specs=pl.BlockSpec((chips, 1, rows // chips, tile), lambda e, f: (0, e, 0, f)),
        cost_estimate=pl.CostEstimate(
            flops=4 * half * rows * width * wide,
            bytes_accessed=4 * half * (rows * width + width * wide) + 2 * half * rows * wide,
            transcendentals=0,
        ),
        compiler_params=pltpu.CompilerParams(vmem_limit_bytes=32 * 1024 * 1024),
        name="partials",
    )(own, other, w_own, w_other)


def expert_out_kernel(
    got_ref, gate_ref, g_own_ref, g_other_ref, w_own_ref, w_other_ref, own_ref, other_ref, dots_ref
):
    rows = got_ref.shape[0] * got_ref.shape[2]
    got = got_ref[...].reshape(rows, got_ref.shape[3])
    gates = gate_ref[0]
    dots = jnp.zeros((rows, 1), jnp.float32)
    for w_ref, g_ref, out_ref in (
        (w_other_ref, g_other_ref, other_ref),
        (w_own_ref, g_own_ref, own_ref),
    ):
        total = jnp.dot(got, w_ref[0], preferred_element_type=jnp.float32)
        grads = g_ref[...].reshape(rows, g_ref.shape[3]).astype(jnp.float32)
        dots = dots + jnp.sum(total * grads, axis=1, keepdims=True)
        out_ref[...] = (total * gates).astype(out_ref.dtype).reshape(out_ref.shape)
    filled = gates > 0
    dots_ref[0] = jnp.where(filled, dots / jnp.where(filled, gates, 1.0), 0.0)


def slot_grad_kernel(got_ref, w_own_ref, w_other_ref, own_ref, other_ref):
    rows = got_ref.shape[0] * got_ref.shape[2]
    got = got_ref[...].reshape(rows, got_ref.shape[3])
    for w_ref, out_ref in ((w_other_ref, other_ref), (w_own_ref, own_ref)):
        total = lax.dot_general(got, w_ref[0], CONTRACT_LAST, preferred_element_type=jnp.float32)
        out_ref[...] = total.astype(out_ref.dtype).reshape(out_ref.shape)


def per_expert(kernel, got, w_own, w_other, cap, width_last, gates=None, grads=()):
    chips, half, share, wide = got.shape
    width = w_own.shape[1] if width_last else w_own.shape[2]
    rows = chips * share
    w_spec = pl.BlockSpec((1,) + w_own.shape[1:], lambda e, p: (e, 0, 0))
    row_spec = pl.BlockSpec((rows // cap // 2, 1, cap, width), lambda e, p: (p, e, 0, 0))
    column_spec = pl.BlockSpec((1, rows // 2, 1), lambda e, p: (e, p, 0))
    outs = [jax.ShapeDtypeStruct((rows // cap, half, cap, width), got.dtype)] * 2
    out_specs = [row_spec, row_spec]
    in_specs = [pl.BlockSpec((chips // 2, 1, share, wide), lambda e, p: (p, e, 0, 0))]
    args = [got]
    if gates is not None:
        in_specs = in_specs + [column_spec, row_spec, row_spec]
        args = args + [gates, *grads]
        outs = outs + [jax.ShapeDtypeStruct((half, rows, 1), jnp.float32)]
        out_specs = out_specs + [column_spec]
    return pl.pallas_call(
        kernel,
        out_shape=outs,
        grid=(half, 2),
        in_specs=in_specs + [w_spec, w_spec],
        out_specs=out_specs,
        cost_estimate=pl.CostEstimate(
            flops=4 * half * rows * width * wide,
            bytes_accessed=2 * half * rows * wide + 4 * half * (width * wide + rows * width),
            transcendentals=0,
        ),
        compiler_params=pltpu.CompilerParams(vmem_limit_bytes=32 * 1024 * 1024),
        name=kernel.__name__,
    )(*args, w_own, w_other)


def merge_kernel(odd_ref, *refs):
    pieces, (keep_ref, give_ref) = refs[:-2], refs[-2:]
    extra = (keep_ref.shape[0] - pieces[0].shape[1]) // (len(pieces) - 1)
    tok = pieces[0].shape[1] - extra
    odd = odd_ref[0] == 1

    def store(rows, values):
        keep_ref[rows] = jnp.where(odd, values[1], values[0])
        give_ref[rows] = jnp.where(odd, values[0], values[1])

    total = pieces[0][:, :tok].astype(jnp.float32)
    for piece in pieces[1:]:
        total = total + piece[:, :tok].astype(jnp.float32)
    store(slice(0, tok), total.astype(keep_ref.dtype))
    for index, piece in enumerate(pieces):
        start = tok + index * extra
        store(slice(start, start + extra), piece[:, tok:])


def merge(odd, pieces, extra):
    tok, width = pieces[0].shape[1] - extra, pieces[0].shape[2]
    out = jax.ShapeDtypeStruct((tok + extra * len(pieces), width), pieces[0].dtype)
    vmem = pl.BlockSpec(memory_space=pltpu.VMEM)
    return pl.pallas_call(
        merge_kernel,
        out_shape=(out, out),
        in_specs=[pl.BlockSpec(memory_space=pltpu.SMEM)] + [vmem] * len(pieces),
        out_specs=(vmem, vmem),
        name="merge",
    )(odd.reshape(1), *pieces)


def three_pieces(value):
    high = lax.reduce_precision(value, 8, 7)
    rest = value - high
    middle = lax.reduce_precision(rest, 8, 7)
    low = rest - middle
    return [piece.astype(jnp.bfloat16) for piece in (high, middle, low)]


def after(value, earlier):
    return lax.optimization_barrier((value, earlier))[0]


def spread(block, axis_name, size, groups=None):
    copies = jnp.broadcast_to(block[None], (size,) + block.shape)
    return lax.all_to_all(copies, axis_name, 0, 0, tiled=True, axis_index_groups=groups)


def on_device(tokens, expert_ids, gate_prob, w_gate, w_up, w_down, grad_out):
    bf16, f32 = jnp.bfloat16, jnp.float32
    tok, fanout = expert_ids.shape
    n_exp, width, ff = w_gate.shape
    cols = lax.axis_size("expert")
    parties = lax.axis_size("dp")
    cap = 2 * tok * fanout // (n_exp * cols)
    half = n_exp // 2
    chips = parties // 2
    per_share = cols // chips
    share = per_share * cap
    core = lax.axis_index("dp") % 2
    col = lax.axis_index("expert")
    mine, theirs = core * half, (1 - core) * half
    pairs = [(i, i ^ 1) for i in range(parties)]
    same_core = [[i for i in range(parties) if i % 2 == c] for c in (0, 1)]

    levels = cols // 2
    level = col // 2

    def shifted(value, step):
        steps = [(i, (i + 2 * step) % cols) for i in range(cols)]
        return lax.ppermute(value, "expert", steps)

    def swap(value):
        return lax.ppermute(value, "dp", pairs)

    def pick(value, start, axis):
        return lax.dynamic_slice_in_dim(value, start, half, axis)

    def packed(rows):
        lanes = width // tok
        each = -(-rows.shape[0] // (8 * lanes)) * 8
        rows = jnp.pad(rows, ((0, each * lanes - rows.shape[0]), (0, 0)))
        return jnp.concatenate([rows[i * each : (i + 1) * each] for i in range(lanes)], axis=1)

    def unpacked(rows, count):
        lanes = width // tok
        parts = [rows[:, :, i * tok : (i + 1) * tok] for i in range(lanes)]
        return jnp.concatenate(parts, axis=1)[:, :count].astype(f32)

    with jax.named_scope("send_tokens"):
        routing = packed(expert_ids.T.astype(bf16))
        got_tokens = spread(jnp.concatenate([tokens, routing], axis=0), "expert", cols)
    with jax.named_scope("send_grads"):
        own_grads = jnp.concatenate(
            [grad_out, packed(jnp.concatenate(three_pieces(gate_prob.T), axis=0))], axis=0
        )
        beside = lax.ppermute(own_grads, "expert", [(i, i ^ 1) for i in range(cols)])
        even = col % 2 == 0
        grad_pair = jnp.stack(
            [jnp.where(even, own_grads, beside), jnp.where(even, beside, own_grads)]
        )

    with jax.named_scope("swap_weights"):
        w_gate_up = jnp.concatenate([w_gate, w_up], axis=2)
        wgu_mine = pick(w_gate_up, mine, 0)
        wgu_theirs = swap(pick(w_gate_up, theirs, 0))
        wd_mine = pick(w_down, mine, 0)
        wd_theirs = swap(pick(w_down, theirs, 0))

    with jax.named_scope("tables"):
        got_tokens = after(got_tokens, (beside, wd_theirs))
        all_tokens = got_tokens[:, :tok]
        ids = unpacked(got_tokens[:, tok:], fanout)
        names = (col * n_exp + jnp.arange(n_exp)).astype(f32)
        chosen = ids[:, None] == names[None, :, None, None]
        hit = jnp.sum(chosen.astype(f32), axis=2)
        earlier = (jnp.arange(tok)[:, None] < jnp.arange(tok)[None, :]).astype(bf16)
        rank = jnp.einsum("sea,at->set", hit.astype(bf16), earlier, preferred_element_type=f32)
        placed = (rank[:, :, None] == jnp.arange(cap, dtype=f32)[None, None, :, None]) & (
            hit[:, :, None] > 0.5
        )
        slots = placed.astype(bf16)

    def dispatch(source):
        return jnp.einsum(
            "sqt,std->sqd",
            slots.reshape(cols, n_exp * cap, tok),
            source,
            preferred_element_type=f32,
        ).reshape(cols, n_exp, cap, width)

    def join_rows(own, other):
        rows = jnp.concatenate([own, other], axis=3).transpose(1, 0, 2, 3)
        return rows.reshape(half, cols * cap, 2 * width)

    def shares(part):
        return lax.all_to_all(part, "dp", 0, 0, tiled=True, axis_index_groups=same_core)

    def total(got):
        return jnp.sum(got.astype(f32), axis=0)

    def in_rows(got):
        return got.transpose(1, 0, 2, 3).reshape(half, chips * share, got.shape[-1])

    with jax.named_scope("gate_up"):
        x_all = dispatch(all_tokens).astype(bf16)
        x_mine = pick(x_all, mine, 1)
        x_theirs = swap(pick(x_all, theirs, 1))
        part = partials(x_mine, x_theirs, wgu_mine, wgu_theirs, chips, False)
        got_gate_up = shares(part)
        gate_up = total(got_gate_up)
        gate_pre, up_pre = gate_up[..., :ff], gate_up[..., ff:]
        sigmoid_g = jax.nn.sigmoid(gate_pre)
        hidden = (gate_pre * sigmoid_g * up_pre).astype(bf16)
        got_hidden = spread(hidden, "dp", chips, same_core)
        grad_pair = after(grad_pair, part)

    with jax.named_scope("all_grads"):
        all_grads = jnp.zeros((cols,) + own_grads.shape, bf16)
        for step in range(levels):
            piece = shifted(grad_pair, step) if step else grad_pair
            start = 2 * ((level + levels - step) % levels)
            all_grads = lax.dynamic_update_slice_in_dim(all_grads, piece, start, 0)

    with jax.named_scope("hidden_grad"):
        gates = unpacked(all_grads[:, tok:], 3 * fanout)
        gates = gates[:, :fanout] + gates[:, fanout : 2 * fanout] + gates[:, 2 * fanout :]
        gate_of = jnp.sum(jnp.where(chosen, gates[:, None], 0.0), axis=2)
        gate_slots = jnp.sum(jnp.where(placed, gate_of[:, :, None], 0.0), axis=3)
        g_all = (dispatch(all_grads[:, :tok]) * gate_slots[..., None]).astype(bf16)
        g_mine = pick(g_all, mine, 1)
        g_theirs = swap(pick(g_all, theirs, 1))
        part = partials(g_mine, g_theirs, wd_mine, wd_theirs, chips, True)
        got = shares(after(part, got_hidden))
        hidden_grad = total(got)
    slots_mine = pick(slots, mine, 1).reshape(cols, half * cap, tok)
    slots_theirs = pick(slots, theirs, 1).reshape(cols, half * cap, tok)

    def combine(own, other):
        def part(slot, value):
            value = value.reshape(cols, half * cap, width)
            return jnp.einsum("sqt,sqd->std", slot, value, preferred_element_type=f32)

        return (part(slots_mine, own) + part(slots_theirs, other)).astype(bf16)

    with jax.named_scope("mixed"):
        row_gates = pick(gate_slots, mine, 1).transpose(1, 0, 2).reshape(half, cols * cap, 1)
        out_own, out_other, dots = per_expert(
            expert_out_kernel, got_hidden, wd_mine, wd_theirs, cap, False, row_gates, (g_mine, g_theirs)
        )
        mixed_parts = combine(out_own, swap(out_other))
        slot_dots = dots.reshape(half, cols, cap).transpose(1, 0, 2)
        dot_of = jnp.sum(jnp.where(pick(placed, mine, 1), slot_dots[..., None], 0.0), axis=2)
        dot_rows = jax.vmap(packed)(jnp.concatenate(three_pieces(dot_of), axis=1))
        extra = dot_rows.shape[1]
        outgoing = jnp.concatenate([mixed_parts, dot_rows], axis=1)
        by_level = outgoing.reshape(levels, 2, tok + extra, width)

        def at_level(step):
            return lax.dynamic_index_in_dim(by_level, (level + step) % levels, 0, keepdims=False)

        arrived = [at_level(0)] + [shifted(at_level(step), step) for step in range(1, levels)]
        keep, give = merge((col % 2).astype(jnp.int32), arrived, extra)
        take = lax.ppermute(give, "expert", [(i, i ^ 1) for i in range(cols)])
        mixed = (keep[:tok].astype(f32) + take[:tok].astype(f32)).astype(bf16)

    with jax.named_scope("local_grads"):
        gate_grad = (hidden_grad * up_pre * sigmoid_g * (1.0 + gate_pre * (1.0 - sigmoid_g))).astype(bf16)
        up_grad = (hidden_grad * gate_pre * sigmoid_g).astype(bf16)
        local_grads = after(jnp.concatenate([gate_grad, up_grad], axis=2), outgoing)
        got_grads = spread(local_grads, "dp", chips, same_core)

    with jax.named_scope("grad_tokens"):
        g_rows = join_rows(g_mine, g_theirs)
        all_hidden = in_rows(after(got_hidden, mixed_parts))
        dd = jnp.einsum("erf,erd->efd", all_hidden, g_rows, preferred_element_type=f32).astype(bf16)
        got_grads = after(got_grads, (take, dd))
        slot_own, slot_other = per_expert(
            slot_grad_kernel, got_grads, wgu_mine, wgu_theirs, cap, True
        )
        grad_parts = after(combine(slot_own, swap(slot_other)), mixed)
        back = lax.all_to_all(grad_parts, "expert", 0, 0, tiled=True)
        grad_tokens = jnp.sum(back.astype(f32), axis=0).astype(bf16)
        gu_grads = in_rows(after(got_grads, grad_parts))

    with jax.named_scope("grad_gate"):
        both = jnp.concatenate([keep[tok:], take[tok:]], axis=0)
        both = unpacked(both.reshape(2 * levels, extra, width), 3 * half)
        values = (both[:, :half] + both[:, half : 2 * half] + both[:, 2 * half :]).reshape(-1, tok)
        from_level = (level + levels - jnp.arange(levels)) % levels
        from_col = jnp.concatenate([2 * from_level + col % 2, 2 * from_level + 1 - col % 2])
        owners = (from_col[:, None] * n_exp + mine + jnp.arange(half)[None, :]).reshape(-1)
        picked = expert_ids.T[:, None] == owners[None, :, None].astype(expert_ids.dtype)
        gate_sum = after(jnp.sum(jnp.where(picked, values[None], 0.0), axis=1), grad_parts)
        bit = 1
        while bit < parties:
            gate_sum = gate_sum + lax.ppermute(gate_sum, "dp", [(i, i ^ bit) for i in range(parties)])
            bit = bit * 2
        grad_gate = gate_sum.T

    def both_halves(own, other):
        out = jnp.zeros((n_exp,) + own.shape[1:], own.dtype)
        out = lax.dynamic_update_slice_in_dim(out, own, mine, 0)
        return lax.dynamic_update_slice_in_dim(out, other, theirs, 0)

    with jax.named_scope("weight_grads"):
        x_rows = join_rows(after(x_mine, grad_parts), x_theirs)
        dd = after(dd, grad_parts)
        dgu = jnp.einsum("erd,erf->edf", x_rows, gu_grads, preferred_element_type=f32).astype(bf16)
        dgu_other = swap(dgu[:, width:])
        dd_other = swap(dd[..., width:])
        grad_w_gate = both_halves(dgu[:, :width, :ff], dgu_other[..., :ff])
        grad_w_up = both_halves(dgu[:, :width, ff:], dgu_other[..., ff:])
        grad_w_down = both_halves(dd[..., :width], dd_other)
    return (mixed, grad_tokens, grad_gate, grad_w_gate, grad_w_up, grad_w_down)


def solution(mesh):
    return jax.shard_map(
        on_device,
        mesh=mesh,
        in_specs=(
            P("expert", "dp"),
            P("expert", None),
            P("expert", None),
            P("expert", "dp", None),
            P("expert", "dp", None),
            P("expert", None, "dp"),
            P("expert", "dp"),
        ),
        out_specs=(
            P("expert", "dp"),
            P("expert", "dp"),
            P("expert", None),
            P("expert", "dp", None),
            P("expert", "dp", None),
            P("expert", None, "dp"),
        ),
        check_vma=False,
    )
```

```python
import functools

import jax
import jax.numpy as jnp
from jax import lax
from jax.experimental import pallas as pl
from jax.experimental.pallas import tpu as pltpu
from jax.sharding import PartitionSpec as P

CONTRACT_LAST = (((1,), (1,)), ((), ()))
CONTRACT_INNER = (((1,), (0,)), ((), ()))


def partials_kernel(contract, own_ref, other_ref, w_own_ref, w_other_ref, out_ref):
    rows = own_ref.shape[0] * own_ref.shape[2]
    own = own_ref[...].reshape(rows, own_ref.shape[3])
    other = other_ref[...].reshape(rows, other_ref.shape[3])
    total = lax.dot_general(own, w_own_ref[0], contract, preferred_element_type=jnp.float32)
    total = total + lax.dot_general(
        other, w_other_ref[0], contract, preferred_element_type=jnp.float32
    )
    out_ref[...] = total.astype(out_ref.dtype).reshape(out_ref.shape)


def partials(own, other, w_own, w_other, chips, width_last):
    blocks, half, cap, width = own.shape
    wide = w_own.shape[1] if width_last else w_own.shape[2]
    tile = wide // 2 if wide % 256 == 0 else wide
    rows = blocks * cap
    row_spec = pl.BlockSpec((blocks, 1, cap, width), lambda e, f: (0, e, 0, 0))
    if width_last:
        w_spec = pl.BlockSpec((1, tile, width), lambda e, f: (e, f, 0))
    else:
        w_spec = pl.BlockSpec((1, width, tile), lambda e, f: (e, 0, f))
    return pl.pallas_call(
        functools.partial(partials_kernel, CONTRACT_LAST if width_last else CONTRACT_INNER),
        out_shape=pltpu.HBM((chips, half, rows // chips, wide), own.dtype),
        grid=(half, wide // tile),
        in_specs=[row_spec, row_spec, w_spec, w_spec],
        out_specs=pl.BlockSpec((chips, 1, rows // chips, tile), lambda e, f: (0, e, 0, f)),
        cost_estimate=pl.CostEstimate(
            flops=4 * half * rows * width * wide,
            bytes_accessed=4 * half * (rows * width + width * wide) + 2 * half * rows * wide,
            transcendentals=0,
        ),
        compiler_params=pltpu.CompilerParams(vmem_limit_bytes=32 * 1024 * 1024),
        name="partials",
    )(own, other, w_own, w_other)


def expert_out_kernel(
    got_ref, gate_ref, g_own_ref, g_other_ref, w_own_ref, w_other_ref, own_ref, other_ref, dots_ref
):
    rows = got_ref.shape[0] * got_ref.shape[2]
    got = got_ref[...].reshape(rows, got_ref.shape[3])
    gates = gate_ref[0]
    dots = jnp.zeros((rows, 1), jnp.float32)
    for w_ref, g_ref, out_ref in (
        (w_other_ref, g_other_ref, other_ref),
        (w_own_ref, g_own_ref, own_ref),
    ):
        total = jnp.dot(got, w_ref[0], preferred_element_type=jnp.float32)
        grads = g_ref[...].reshape(rows, g_ref.shape[3]).astype(jnp.float32)
        dots = dots + jnp.sum(total * grads, axis=1, keepdims=True)
        out_ref[...] = (total * gates).astype(out_ref.dtype).reshape(out_ref.shape)
    filled = gates > 0
    dots_ref[0] = jnp.where(filled, dots / jnp.where(filled, gates, 1.0), 0.0)


def slot_grad_kernel(got_ref, w_own_ref, w_other_ref, own_ref, other_ref):
    rows = got_ref.shape[0] * got_ref.shape[2]
    got = got_ref[...].reshape(rows, got_ref.shape[3])
    for w_ref, out_ref in ((w_other_ref, other_ref), (w_own_ref, own_ref)):
        total = lax.dot_general(got, w_ref[0], CONTRACT_LAST, preferred_element_type=jnp.float32)
        out_ref[...] = total.astype(out_ref.dtype).reshape(out_ref.shape)


def per_expert(kernel, got, w_own, w_other, cap, width_last, gates=None, grads=()):
    split = 1 if gates is None else 2
    chips, half, share, wide = got.shape
    width = w_own.shape[1] if width_last else w_own.shape[2]
    rows = chips * share
    w_spec = pl.BlockSpec((1,) + w_own.shape[1:], lambda e, p: (e, 0, 0))
    row_spec = pl.BlockSpec((rows // cap // split, 1, cap, width), lambda e, p: (p, e, 0, 0))
    column_spec = pl.BlockSpec((1, rows // split, 1), lambda e, p: (e, p, 0))
    outs = [jax.ShapeDtypeStruct((rows // cap, half, cap, width), got.dtype)] * 2
    out_specs = [row_spec, row_spec]
    in_specs = [pl.BlockSpec((chips // split, 1, share, wide), lambda e, p: (p, e, 0, 0))]
    args = [got]
    if gates is not None:
        in_specs = in_specs + [column_spec, row_spec, row_spec]
        args = args + [gates, *grads]
        outs = outs + [jax.ShapeDtypeStruct((half, rows, 1), jnp.float32)]
        out_specs = out_specs + [column_spec]
    return pl.pallas_call(
        kernel,
        out_shape=outs,
        grid=(half, split),
        in_specs=in_specs + [w_spec, w_spec],
        out_specs=out_specs,
        cost_estimate=pl.CostEstimate(
            flops=4 * half * rows * width * wide,
            bytes_accessed=2 * half * rows * wide + 4 * half * (width * wide + rows * width),
            transcendentals=0,
        ),
        compiler_params=pltpu.CompilerParams(vmem_limit_bytes=32 * 1024 * 1024),
        name=kernel.__name__,
    )(*args, w_own, w_other)


def merge_kernel(odd_ref, *refs):
    pieces, (keep_ref, give_ref) = refs[:-2], refs[-2:]
    extra = (keep_ref.shape[0] - pieces[0].shape[1]) // (len(pieces) - 1)
    tok = pieces[0].shape[1] - extra
    odd = odd_ref[0] == 1

    def store(rows, values):
        keep_ref[rows] = jnp.where(odd, values[1], values[0])
        give_ref[rows] = jnp.where(odd, values[0], values[1])

    total = pieces[0][:, :tok].astype(jnp.float32)
    for piece in pieces[1:]:
        total = total + piece[:, :tok].astype(jnp.float32)
    store(slice(0, tok), total.astype(keep_ref.dtype))
    for index, piece in enumerate(pieces):
        start = tok + index * extra
        store(slice(start, start + extra), piece[:, tok:])


def merge(odd, pieces, extra):
    tok, width = pieces[0].shape[1] - extra, pieces[0].shape[2]
    out = jax.ShapeDtypeStruct((tok + extra * len(pieces), width), pieces[0].dtype)
    vmem = pl.BlockSpec(memory_space=pltpu.VMEM)
    return pl.pallas_call(
        merge_kernel,
        out_shape=(out, out),
        in_specs=[pl.BlockSpec(memory_space=pltpu.SMEM)] + [vmem] * len(pieces),
        out_specs=(vmem, vmem),
        name="merge",
    )(odd.reshape(1), *pieces)


def three_pieces(value):
    high = lax.reduce_precision(value, 8, 7)
    rest = value - high
    middle = lax.reduce_precision(rest, 8, 7)
    low = rest - middle
    return [piece.astype(jnp.bfloat16) for piece in (high, middle, low)]


def after(value, earlier):
    return lax.optimization_barrier((value, earlier))[0]


def spread(block, axis_name, size, groups=None):
    copies = jnp.broadcast_to(block[None], (size,) + block.shape)
    return lax.all_to_all(copies, axis_name, 0, 0, tiled=True, axis_index_groups=groups)


def on_device(tokens, expert_ids, gate_prob, w_gate, w_up, w_down, grad_out):
    bf16, f32 = jnp.bfloat16, jnp.float32
    tok, fanout = expert_ids.shape
    n_exp, width, ff = w_gate.shape
    cols = lax.axis_size("expert")
    parties = lax.axis_size("dp")
    cap = 2 * tok * fanout // (n_exp * cols)
    half = n_exp // 2
    chips = parties // 2
    per_share = cols // chips
    share = per_share * cap
    core = lax.axis_index("dp") % 2
    col = lax.axis_index("expert")
    mine, theirs = core * half, (1 - core) * half
    pairs = [(i, i ^ 1) for i in range(parties)]
    same_core = [[i for i in range(parties) if i % 2 == c] for c in (0, 1)]

    levels = cols // 2
    level = col // 2

    def shifted(value, step):
        steps = [(i, (i + 2 * step) % cols) for i in range(cols)]
        return lax.ppermute(value, "expert", steps)

    def swap(value):
        return lax.ppermute(value, "dp", pairs)

    def pick(value, start, axis):
        return lax.dynamic_slice_in_dim(value, start, half, axis)

    def packed(rows):
        lanes = width // tok
        each = -(-rows.shape[0] // (8 * lanes)) * 8
        rows = jnp.pad(rows, ((0, each * lanes - rows.shape[0]), (0, 0)))
        return jnp.concatenate([rows[i * each : (i + 1) * each] for i in range(lanes)], axis=1)

    def unpacked(rows, count):
        lanes = width // tok
        parts = [rows[:, :, i * tok : (i + 1) * tok] for i in range(lanes)]
        return jnp.concatenate(parts, axis=1)[:, :count].astype(f32)

    with jax.named_scope("send_tokens"):
        routing = packed(expert_ids.T.astype(bf16))
        got_tokens = spread(jnp.concatenate([tokens, routing], axis=0), "expert", cols)
    with jax.named_scope("send_grads"):
        own_grads = jnp.concatenate(
            [grad_out, packed(jnp.concatenate(three_pieces(gate_prob.T), axis=0))], axis=0
        )
        beside = lax.ppermute(own_grads, "expert", [(i, i ^ 1) for i in range(cols)])
        even = col % 2 == 0
        grad_pair = jnp.stack(
            [jnp.where(even, own_grads, beside), jnp.where(even, beside, own_grads)]
        )

    with jax.named_scope("swap_weights"):
        w_gate_up = jnp.concatenate([w_gate, w_up], axis=2)
        wgu_mine = pick(w_gate_up, mine, 0)
        wgu_theirs = swap(pick(w_gate_up, theirs, 0))
        wd_mine = pick(w_down, mine, 0)
        wd_theirs = swap(pick(w_down, theirs, 0))

    with jax.named_scope("tables"):
        got_tokens = after(got_tokens, (beside, wd_theirs))
        all_tokens = got_tokens[:, :tok]
        ids = unpacked(got_tokens[:, tok:], fanout)
        names = (col * n_exp + jnp.arange(n_exp)).astype(f32)
        chosen = ids[:, None] == names[None, :, None, None]
        hit = jnp.sum(chosen.astype(f32), axis=2)
        earlier = (jnp.arange(tok)[:, None] < jnp.arange(tok)[None, :]).astype(bf16)
        rank = jnp.einsum("sea,at->set", hit.astype(bf16), earlier, preferred_element_type=f32)
        placed = (rank[:, :, None] == jnp.arange(cap, dtype=f32)[None, None, :, None]) & (
            hit[:, :, None] > 0.5
        )
        slots = placed.astype(bf16)

    def dispatch(source):
        return jnp.einsum(
            "sqt,std->sqd",
            slots.reshape(cols, n_exp * cap, tok),
            source,
            preferred_element_type=f32,
        ).reshape(cols, n_exp, cap, width)

    def join_rows(own, other):
        rows = jnp.concatenate([own, other], axis=3).transpose(1, 0, 2, 3)
        return rows.reshape(half, cols * cap, 2 * width)

    def shares(part):
        return lax.all_to_all(part, "dp", 0, 0, tiled=True, axis_index_groups=same_core)

    def total(got):
        return jnp.sum(got.astype(f32), axis=0)

    def in_rows(got):
        return got.transpose(1, 0, 2, 3).reshape(half, chips * share, got.shape[-1])

    with jax.named_scope("gate_up"):
        x_all = dispatch(all_tokens).astype(bf16)
        x_mine = pick(x_all, mine, 1)
        x_theirs = swap(pick(x_all, theirs, 1))
        part = partials(x_mine, x_theirs, wgu_mine, wgu_theirs, chips, False)
        got_gate_up = shares(part)
        gate_up = total(got_gate_up)
        gate_pre, up_pre = gate_up[..., :ff], gate_up[..., ff:]
        sigmoid_g = jax.nn.sigmoid(gate_pre)
        hidden = (gate_pre * sigmoid_g * up_pre).astype(bf16)
        got_hidden = spread(hidden, "dp", chips, same_core)
        grad_pair = after(grad_pair, part)

    with jax.named_scope("all_grads"):
        all_grads = jnp.zeros((cols,) + own_grads.shape, bf16)
        for step in range(levels):
            piece = shifted(grad_pair, step) if step else grad_pair
            start = 2 * ((level + levels - step) % levels)
            all_grads = lax.dynamic_update_slice_in_dim(all_grads, piece, start, 0)

    with jax.named_scope("hidden_grad"):
        gates = unpacked(all_grads[:, tok:], 3 * fanout)
        gates = gates[:, :fanout] + gates[:, fanout : 2 * fanout] + gates[:, 2 * fanout :]
        gate_of = jnp.sum(jnp.where(chosen, gates[:, None], 0.0), axis=2)
        gate_slots = jnp.sum(jnp.where(placed, gate_of[:, :, None], 0.0), axis=3)
        g_all = (dispatch(all_grads[:, :tok]) * gate_slots[..., None]).astype(bf16)
        g_mine = pick(g_all, mine, 1)
        g_theirs = swap(pick(g_all, theirs, 1))
        part = partials(g_mine, g_theirs, wd_mine, wd_theirs, chips, True)
        got = shares(after(part, got_hidden))
        hidden_grad = total(got)
    slots_mine = pick(slots, mine, 1).reshape(cols, half * cap, tok)
    slots_theirs = pick(slots, theirs, 1).reshape(cols, half * cap, tok)

    def combine(own, other):
        def part(slot, value):
            value = value.reshape(cols, half * cap, width)
            return jnp.einsum("sqt,sqd->std", slot, value, preferred_element_type=f32)

        return (part(slots_mine, own) + part(slots_theirs, other)).astype(bf16)

    with jax.named_scope("mixed"):
        row_gates = pick(gate_slots, mine, 1).transpose(1, 0, 2).reshape(half, cols * cap, 1)
        out_own, out_other, dots = per_expert(
            expert_out_kernel, got_hidden, wd_mine, wd_theirs, cap, False, row_gates, (g_mine, g_theirs)
        )
        mixed_parts = combine(out_own, swap(out_other))
        slot_dots = dots.reshape(half, cols, cap).transpose(1, 0, 2)
        dot_of = jnp.sum(jnp.where(pick(placed, mine, 1), slot_dots[..., None], 0.0), axis=2)
        dot_rows = jax.vmap(packed)(jnp.concatenate(three_pieces(dot_of), axis=1))
        extra = dot_rows.shape[1]
        outgoing = jnp.concatenate([mixed_parts, dot_rows], axis=1)
        by_level = outgoing.reshape(levels, 2, tok + extra, width)

        def at_level(step):
            return lax.dynamic_index_in_dim(by_level, (level + step) % levels, 0, keepdims=False)

        arrived = [at_level(0)] + [shifted(at_level(step), step) for step in range(1, levels)]
        g_rows = join_rows(g_mine, g_theirs)
        all_hidden = in_rows(after(got_hidden, arrived[1]))
        dd = jnp.einsum("erf,erd->efd", all_hidden, g_rows, preferred_element_type=f32).astype(bf16)
        arrived[0] = after(arrived[0], dd)
        keep, give = merge((col % 2).astype(jnp.int32), arrived, extra)
        take = lax.ppermute(give, "expert", [(i, i ^ 1) for i in range(cols)])

    with jax.named_scope("local_grads"):
        gate_grad = (hidden_grad * up_pre * sigmoid_g * (1.0 + gate_pre * (1.0 - sigmoid_g))).astype(bf16)
        up_grad = (hidden_grad * gate_pre * sigmoid_g).astype(bf16)
        local_grads = after(jnp.concatenate([gate_grad, up_grad], axis=2), outgoing)
        got_grads = spread(local_grads, "dp", chips, same_core)

    with jax.named_scope("grad_tokens"):
        got_grads = after(got_grads, take)
        slot_own, slot_other = per_expert(
            slot_grad_kernel, got_grads, wgu_mine, wgu_theirs, cap, True
        )
        grad_parts = combine(slot_own, swap(slot_other))
        keep, take = after((keep, take), grad_parts)
        mixed = (keep[:tok].astype(f32) + take[:tok].astype(f32)).astype(bf16)
        back = lax.all_to_all(grad_parts, "expert", 0, 0, tiled=True)
        grad_tokens = jnp.sum(back.astype(f32), axis=0).astype(bf16)
        gu_grads = in_rows(after(got_grads, grad_parts))

    with jax.named_scope("grad_gate"):
        both = jnp.concatenate([keep[tok:], take[tok:]], axis=0)
        both = unpacked(both.reshape(2 * levels, extra, width), 3 * half)
        values = (both[:, :half] + both[:, half : 2 * half] + both[:, 2 * half :]).reshape(-1, tok)
        from_level = (level + levels - jnp.arange(levels)) % levels
        from_col = jnp.concatenate([2 * from_level + col % 2, 2 * from_level + 1 - col % 2])
        owners = (from_col[:, None] * n_exp + mine + jnp.arange(half)[None, :]).reshape(-1)
        picked = expert_ids.T[:, None] == owners[None, :, None].astype(expert_ids.dtype)
        gate_sum = after(jnp.sum(jnp.where(picked, values[None], 0.0), axis=1), grad_parts)
        bit = 1
        while bit < parties:
            gate_sum = gate_sum + lax.ppermute(gate_sum, "dp", [(i, i ^ bit) for i in range(parties)])
            bit = bit * 2
        grad_gate = gate_sum.T

    def both_halves(own, other):
        out = jnp.zeros((n_exp,) + own.shape[1:], own.dtype)
        out = lax.dynamic_update_slice_in_dim(out, own, mine, 0)
        return lax.dynamic_update_slice_in_dim(out, other, theirs, 0)

    with jax.named_scope("weight_grads"):
        x_rows = join_rows(after(x_mine, grad_parts), x_theirs)
        dd = after(dd, grad_parts)
        dgu = jnp.einsum("erd,erf->edf", x_rows, gu_grads, preferred_element_type=f32).astype(bf16)
        dgu_other = swap(dgu[:, width:])
        dd_other = swap(dd[..., width:])
        grad_w_gate = both_halves(dgu[:, :width, :ff], dgu_other[..., :ff])
        grad_w_up = both_halves(dgu[:, :width, ff:], dgu_other[..., ff:])
        grad_w_down = both_halves(dd[..., :width], dd_other)
    return (mixed, grad_tokens, grad_gate, grad_w_gate, grad_w_up, grad_w_down)


def solution(mesh):
    return jax.shard_map(
        on_device,
        mesh=mesh,
        in_specs=(
            P("expert", "dp"),
            P("expert", None),
            P("expert", None),
            P("expert", "dp", None),
            P("expert", "dp", None),
            P("expert", None, "dp"),
            P("expert", "dp"),
        ),
        out_specs=(
            P("expert", "dp"),
            P("expert", "dp"),
            P("expert", None),
            P("expert", "dp", None),
            P("expert", "dp", None),
            P("expert", None, "dp"),
        ),
        check_vma=False,
    )
```
